256 devices in a mesh: gx: 16 (over y, x_lo, core), yz: 16 (over z, x_hi).
Axes of the slice: x: 4 (x_hi: 2, x_lo: 2; x = x_hi * 2 + x_lo), y: 4, z: 8, core: 2. Of those that a mesh axis runs over, the one named last changes fastest.
Arguments:
- a_blocks: bfloat16 [4096, 64, 448], P(('gx', 'yz')), may hold values from -0.75 to 0.75
- p_blocks: bfloat16 [4096, 64, 192], P(('gx', 'yz')), may hold values from -0.75 to 0.75
- a_slot: int32 [4096, 7], P(('gx', 'yz')), may hold values from 0 to 31
- halo_rows: int32 [256, 4, 4], P(('gx', 'yz')), may hold values from 0 to 15
- p_cols: int32 [4096, 3], P(('gx', 'yz')), may hold values from 0 to 8, as said below
- t_slot: int32 [4096, 3, 7, 3], P(('gx', 'yz')), may hold values from 0 to 8
Outputs:
- coarse: float32 [512, 64, 576], P(('gx', 'yz'))
The draws below stay inside these ranges and needn't reach their ends.
Inputs may be any that keep to these rules, and one draw needn't show every extreme that they name: `a_slot`: values below 16 name the device's own element rows; a value v of 16 or more names entry (v - 16) % 4 of the list for neighbour (v - 16) // 4. `halo_rows`: entry [d, k, h] is a local row index on the k-th neighbour of device d. `p_cols`: value r names local aggregate r % 2 of the device itself if r // 2 = 0, else local aggregate r % 2 of its neighbour number r // 2 - 1, and then r % 2 is below 1.
All inputs are finite; a program needn't handle non-finite values.
Results may differ from the reference program's by a relative error of at most 0.004.
Values may be sent and summed in bfloat16 or wider, within the bound.
No kernel may reach another device: no remote copies, remote signals or barrier semaphores. Data moves between devices by JAX's collectives and lax.ppermute only.
A program may use at most 128 MiB of HBM per device.

```python
import jax
import jax.numpy as jnp
from jax import lax

B = 64
CB = 64
KA = 7
KP = 3
KC = 9
E_DEV = 16
HALO = 4
AGG_DEV = 2
BAGG = 1
NE = 4096
NC = 512
N_GX = 16
N_YZ = 16


def draw_p_cols(key, part):
    keys = jax.random.split(jax.random.fold_in(key, 7), 4)
    own = jax.random.randint(keys[0], (NE, KP), 0, AGG_DEV)
    picked = jax.random.randint(keys[1], (NE, KP), 0, 8)
    heading = jax.random.randint(keys[2], (NE, KP), 0, 4)
    named = jax.random.randint(keys[3], (NE, KP), 0, BAGG)
    far = (heading + 1) * AGG_DEV + named
    local = jnp.arange(NE, dtype=jnp.int32) % E_DEV
    forced = (local < 4)[:, None] & (jnp.arange(KP, dtype=jnp.int32) == 0)[None, :]
    far_forced = (local[:, None] + 1) * AGG_DEV + named
    result = jnp.where(forced, far_forced, jnp.where(picked == 0, far, own))
    result = result.at[3, 0].set(4 * AGG_DEV + BAGG - 1).at[4, 0].set(0)
    return result.astype(jnp.int32)


def with_ends(values, rng, least, top_value):
    spot = [jax.random.randint(jax.random.fold_in(rng, axis), (), 0, length) for axis, length in enumerate(values.shape)]
    longest = values.shape.index(max(values.shape))
    beside = spot[:longest] + [(spot[longest] + 1) % values.shape[longest]] + spot[longest + 1:]
    return values.at[tuple(spot)].set(least).at[tuple(beside)].set(top_value)


def level_of(key, extent, shards, least, largest):
    gain, own = 1.0, jax.random.fold_in(key, 6)
    for axis_at, shards_of in shards:
        steps = jnp.exp(jax.random.uniform(jax.random.fold_in(own, axis_at), (shards_of,), jnp.float32, least / len(shards), largest / len(shards)))
        gain = gain * jnp.repeat(steps, extent[axis_at] // shards_of).reshape([-1 if axis == axis_at else 1 for axis in range(len(extent))])
    return gain


def normal_values(stream_key, dims, spread, reach, cuts=(), kind=jnp.bfloat16):
    loudness = level_of(stream_key, dims, cuts, -0.22, 0.18) if cuts else 1.0
    entries = jax.random.normal(stream_key, dims, jnp.float32) * spread * loudness
    return jnp.minimum(jnp.maximum(entries, -reach), reach).astype(kind)


def setup_inputs(seed: int = 0) -> dict:
    arg_keys = jax.random.split(jax.random.key(seed), 7)
    a_blocks = normal_values(arg_keys[0], (NE, B, KA * B), B ** -0.5, 0.75, ((0, 256),))
    p_blocks = normal_values(arg_keys[1], (NE, B, KP * CB), B ** -0.5, 0.75, ((0, 256),))
    a_slot = with_ends(jax.random.randint(arg_keys[2], (NE, KA), 0, E_DEV + 4 * HALO), jax.random.fold_in(arg_keys[2], 1), 0, (E_DEV + 4 * HALO) - 1).astype(jnp.int32)
    halo_rows = with_ends(jax.random.randint(arg_keys[3], (N_GX * N_YZ, 4, HALO), 0, E_DEV), jax.random.fold_in(arg_keys[3], 1), 0, E_DEV - 1).astype(jnp.int32)
    p_cols = draw_p_cols(jax.random.fold_in(arg_keys[6], 71), 0)
    t_slot = with_ends(jax.random.randint(arg_keys[5], (NE, KP, KA, KP), 0, KC), jax.random.fold_in(arg_keys[5], 1), 0, KC - 1).astype(jnp.int32)
    return {"a_blocks": a_blocks, "p_blocks": p_blocks, "a_slot": a_slot, "halo_rows": halo_rows, "p_cols": p_cols, "t_slot": t_slot}


def reference(a_blocks, p_blocks, a_slot, halo_rows, p_cols, t_slot):
    device_count = N_GX * N_YZ

    def per_device(coarse_all, device):
        grid_x = device // N_YZ
        grid_yz = device % N_YZ
        sources = jnp.stack([((grid_x - 1) % N_GX) * N_YZ + grid_yz,
                             ((grid_x + 1) % N_GX) * N_YZ + grid_yz,
                             grid_x * N_YZ + (grid_yz - 1) % N_YZ,
                             grid_x * N_YZ + (grid_yz + 1) % N_YZ]).astype(jnp.int32)
        start = (device * E_DEV).astype(jnp.int32)
        slots = lax.dynamic_slice_in_dim(a_slot, start, E_DEV, 0)
        lists = lax.dynamic_index_in_dim(halo_rows, device, 0, keepdims=False)
        halo_index = jnp.clip(slots - E_DEV, 0, 4 * HALO - 1)
        direction = halo_index // HALO
        within = halo_index % HALO
        remote = sources[direction] * E_DEV + lists[direction, within]
        columns = jnp.where(slots < E_DEV, start + slots, remote).astype(jnp.int32)
        fetched = p_blocks[columns]
        own_a = lax.dynamic_slice_in_dim(a_blocks, start, E_DEV, 0).reshape(E_DEV, B, KA, B)
        own_p = lax.dynamic_slice_in_dim(p_blocks, start, E_DEV, 0)
        own_cols = lax.dynamic_slice_in_dim(p_cols, start, E_DEV, 0)
        own_slot = lax.dynamic_slice_in_dim(t_slot, start, E_DEV, 0)
        product = jnp.einsum('ixay,iayz->iaxz', own_a.astype(jnp.float32), fetched.astype(jnp.float32)).astype(jnp.bfloat16)
        product = product.reshape(E_DEV, KA, B, KP, CB)
        owners = jnp.concatenate([jnp.stack([device]).astype(jnp.int32), sources])
        for qidx in range(KP):
            onehot = (own_slot[:, qidx][..., None] == jnp.arange(KC, dtype=jnp.int32)).astype(jnp.float32)
            grouped = jnp.einsum('iaps,iaxpz->isxz', onehot, product.astype(jnp.float32)).astype(jnp.bfloat16)
            p_part = own_p[:, :, qidx * CB:(qidx + 1) * CB]
            term = jnp.einsum('ixw,isxz->iswz', p_part.astype(jnp.float32), grouped.astype(jnp.float32))
            target = owners[own_cols[:, qidx] // AGG_DEV] * AGG_DEV + own_cols[:, qidx] % AGG_DEV
            coarse_all = coarse_all.at[target.astype(jnp.int32)].add(term)
        return coarse_all, None

    initial = jnp.zeros((NC, KC, CB, CB), jnp.float32)
    coarse_all, unused = lax.scan(per_device, initial, jnp.arange(device_count, dtype=jnp.int32))
    return coarse_all.transpose(0, 2, 1, 3).reshape(NC, CB, KC * CB)
```

```python
import jax
import jax.numpy as jnp
from jax import lax
from jax.experimental import pallas as pl
from jax.experimental.pallas import tpu as pltpu
from jax.sharding import PartitionSpec as P

KC = 9
HALF = 32
OWN = 2
F32 = jnp.float32
BF16 = jnp.bfloat16
VMEM = pl.BlockSpec(memory_space=pltpu.VMEM)
SMEM = pl.BlockSpec(memory_space=pltpu.SMEM)


def params(mib=16):
    return pltpu.CompilerParams(vmem_limit_bytes=mib << 20)


def cost(flops, moved):
    return pl.CostEstimate(flops=flops, bytes_accessed=moved, transcendentals=0)


def swapped(value, axis, odd):
    count = lax.axis_size(axis)
    pairs = []
    for low in range(odd, count + odd, 2):
        first, second = low % count, (low + 1) % count
        pairs += [(first, second), (second, first)]
    return lax.ppermute(value, axis, pairs)


def gather_rows(sides, cross, near, far, p_blocks, to_cross, to_near, to_far):
    side_g, side_y = sides[0], sides[1]
    for asked, row, out in ((cross, 1 - side_g, to_cross), (near, 2 + side_y, to_near), (far, 3 - side_y, to_far)):
        for h in range(4):
            out[h] = p_blocks[asked[0, row, h]]


def doubled(block):
    return jnp.concatenate([block, block], axis=1)


def spread(rows, out, index):
    lane = lax.broadcasted_iota(jnp.int32, (64, 128), 1)
    low = lane < 64
    for p in range(3):
        wide = doubled(rows[:, p * 64 : (p + 1) * 64])
        zero = jnp.zeros_like(wide)
        out[index, 0:64, p * 128 : (p + 1) * 128] = jnp.where(low, wide, zero)
        out[index, 64:128, p * 128 : (p + 1) * 128] = jnp.where(low, zero, wide)


def restrict(a_blocks, p_blocks, left, local):
    def body(i, carry):
        rows = p_blocks[i]
        spread(rows, local, i)
        full = lax.dot_general(rows, a_blocks[i], (((0,), (0,)), ((), ())), preferred_element_type=F32).astype(BF16)
        top = jnp.concatenate([full[q * 64 : q * 64 + 32] for q in range(3)], axis=0)
        bottom = jnp.concatenate([full[q * 64 + 32 : q * 64 + 64] for q in range(3)], axis=0)
        for a in range(7):
            left[i, :, a * 128 : (a + 1) * 128] = jnp.concatenate(
                [top[:, a * 64 : (a + 1) * 64], bottom[:, a * 64 : (a + 1) * 64]], axis=1
            )
        return carry

    lax.fori_loop(0, 16, body, 0)


def outward(table, sides, wanted, left, local, chip, cross, near, far, o0, o1, o2, o3, halo, acc0, acc1, acc2):
    accs = (acc0, acc1, acc2)
    for acc in accs:
        acc[...] = jnp.zeros_like(acc)
    row = 1 - sides[0]
    for h in range(4):
        spread(chip[wanted[0, row, h]], halo, h)
        spread(cross[h], halo, 4 + h)
        spread(near[h], halo, 8 + h)
        spread(far[h], halo, 12 + h)

    def body(i, carry):
        for q in range(3):

            @pl.when(table[i, 70 + q] >= OWN)
            def _():
                for a in range(7):
                    slot = table[i, 63 + a]
                    piece = left[i, q * HALF : (q + 1) * HALF, a * 128 : (a + 1) * 128]
                    right = jnp.where(slot < 16, local[jnp.minimum(slot, 15)], halo[jnp.maximum(slot - 16, 0)])
                    value = jnp.dot(piece, right, preferred_element_type=F32)
                    for p in range(3):
                        where = table[i, (q * 7 + a) * 3 + p] - OWN * KC
                        accs[p][where] = accs[p][where] + value[:, p * 128 : (p + 1) * 128]

        return carry

    lax.fori_loop(0, 16, body, 0)
    for k, out in enumerate((o0, o1, o2, o3)):
        part = slice(k * KC, (k + 1) * KC)
        out[...] = (acc0[part] + acc1[part] + acc2[part]).astype(BF16)


def inward(table, left, local, halo, out, acc0, acc1, acc2):
    accs = (acc0, acc1, acc2)
    for acc in accs:
        acc[...] = jnp.zeros_like(acc)

    def body(i, carry):
        for a in range(7):
            slot = table[i, 63 + a]
            right = jnp.where(slot < 16, local[jnp.minimum(slot, 15)], halo[jnp.maximum(slot - 16, 0)])
            value = jnp.dot(left[i, :, a * 128 : (a + 1) * 128], right, preferred_element_type=F32)
            for q in range(3):
                for p in range(3):
                    where = jnp.minimum(table[i, (q * 7 + a) * 3 + p], OWN * KC)
                    accs[p][where] = accs[p][where] + value[q * HALF : (q + 1) * HALF, p * 128 : (p + 1) * 128]
        return carry

    lax.fori_loop(0, 16, body, 0)
    part = slice(0, OWN * KC)
    out[...] = acc0[part] + acc1[part] + acc2[part]


def finish(own, r0, r1, r2, r3, out):
    for c in range(OWN):
        for s in range(KC):
            value = own[c * KC + s]
            if c == 0:
                for r in (r0, r1, r2, r3):
                    value = value + r[s].astype(F32)
            out[c, 0:HALF, s * 64 : (s + 1) * 64] = value[:, 0:64]
            out[c, HALF:64, s * 64 : (s + 1) * 64] = value[:, 64:128]


def shards(a_blocks, p_blocks, a_slot, halo_rows, p_cols, t_slot):
    side_g = lax.axis_index("gx") % 2
    side_y = lax.axis_index("yz") % 2
    sides = jnp.stack([side_g, side_y]).astype(jnp.int32)
    cross_ask = swapped(halo_rows, "gx", 1)
    near_ask = swapped(halo_rows, "yz", 0)
    far_ask = swapped(halo_rows, "yz", 1)
    chip = swapped(p_blocks, "gx", 0)

    flip_g, flip_y = 4 * (1 - side_g), 4 * (1 - side_y)
    slots = jnp.where(a_slot < 16, a_slot, a_slot ^ jnp.where(a_slot < 24, flip_g, flip_y))
    heading = (p_cols // 2 - 1) * 4
    heading = (heading ^ jnp.where(heading < 8, flip_g, flip_y)) // 4
    target = jnp.where(p_cols < 2, p_cols, 2 + heading)
    bins = (target[:, :, None, None] * KC + t_slot).reshape(16, 63)
    table = jnp.concatenate([bins, slots, target], axis=1)

    piece = jax.ShapeDtypeStruct((4, 64, 192), BF16)
    to_cross, to_near, to_far = pl.pallas_call(
        gather_rows, out_shape=[piece] * 3, in_specs=[SMEM] * 4 + [VMEM], out_specs=[VMEM] * 3,
        compiler_params=params(2), cost_estimate=cost(0, 700000), name="gather_rows",
    )(sides, cross_ask, near_ask, far_ask, p_blocks)
    cross = swapped(to_cross, "gx", 1)
    near = swapped(to_near, "yz", 0)
    far = swapped(to_far, "yz", 1)

    left, local = pl.pallas_call(
        restrict,
        out_shape=[jax.ShapeDtypeStruct((16, 96, 896), BF16), jax.ShapeDtypeStruct((16, 128, 384), BF16)],
        in_specs=[VMEM] * 2, out_specs=[VMEM] * 2,
        compiler_params=params(), cost_estimate=cost(400000000, 6000000), name="restrict",
    )(a_blocks, p_blocks)

    packed = jax.ShapeDtypeStruct((KC, HALF, 128), BF16)
    outs = pl.pallas_call(
        outward,
        out_shape=[packed] * 4 + [jax.ShapeDtypeStruct((16, 128, 384), BF16)],
        in_specs=[SMEM] * 3 + [VMEM] * 6, out_specs=[VMEM] * 5,
        scratch_shapes=[pltpu.VMEM((4 * KC, HALF, 128), F32)] * 3,
        compiler_params=params(), cost_estimate=cost(400000000, 6000000), name="outward",
    )(table, sides, halo_rows, left, local, chip, cross, near, far)
    halo = outs[4]
    got = [swapped(outs[0], "gx", 0), swapped(outs[1], "gx", 1), swapped(outs[2], "yz", 0), swapped(outs[3], "yz", 1)]

    own = pl.pallas_call(
        inward,
        out_shape=jax.ShapeDtypeStruct((OWN * KC, HALF, 128), F32),
        in_specs=[SMEM] + [VMEM] * 3, out_specs=VMEM,
        scratch_shapes=[pltpu.VMEM((OWN * KC + 1, HALF, 128), F32)] * 3,
        compiler_params=params(), cost_estimate=cost(1000000000, 8000000), name="inward",
    )(table, left, local, halo)

    return pl.pallas_call(
        finish,
        out_shape=jax.ShapeDtypeStruct((OWN, 64, KC * 64), F32),
        in_specs=[VMEM] * 5, out_specs=VMEM,
        compiler_params=params(4), cost_estimate=cost(0, 1000000), name="finish",
    )(own, *got)


def solution(mesh):
    placed = (
        P(("gx", "yz"), None, None),
        P(("gx", "yz"), None, None),
        P(("gx", "yz"), None),
        P(("gx", "yz"), None, None),
        P(("gx", "yz"), None),
        P(("gx", "yz"), None, None, None),
    )
    return jax.shard_map(
        shards, mesh=mesh, in_specs=placed, out_specs=P(("gx", "yz"), None, None), check_vma=False
    )
```

```python
import jax
import jax.numpy as jnp
from jax import lax
from jax.experimental import pallas as pl
from jax.experimental.pallas import tpu as pltpu
from jax.sharding import PartitionSpec as P


KC = 9
HALF = 32
OWN = 2
BINS = 6 * KC
F32 = jnp.float32
BF16 = jnp.bfloat16
VMEM = pl.BlockSpec(memory_space=pltpu.VMEM)
SMEM = pl.BlockSpec(memory_space=pltpu.SMEM)
ANY = pl.BlockSpec(memory_space=pl.ANY)
HBM = pl.BlockSpec(memory_space=pltpu.HBM)
GROUP = 14
AHEAD = 2
LEFT = jax.ShapeDtypeStruct((128, 96, 128), BF16)
RIGHT = jax.ShapeDtypeStruct((32, 3, 128, 128), BF16)
SUMS = [jax.ShapeDtypeStruct((BINS, HALF, 128), F32)] * 3


def params(mib=16):
    return pltpu.CompilerParams(vmem_limit_bytes=mib << 20)


def cost(flops, moved):
    return pl.CostEstimate(flops=flops, bytes_accessed=moved, transcendentals=0)


def swapped(value, axis, odd):
    count = lax.axis_size(axis)
    pairs = []
    for low in range(odd, count + odd, 2):
        first, second = low % count, (low + 1) % count
        pairs += [(first, second), (second, first)]
    return lax.ppermute(value, axis, pairs)


def gather_rows(sides, cross, near, far, p_blocks, to_cross, to_near, to_far):
    side_g, side_y = sides[0], sides[1]
    for asked, row, out in ((far, 3 - side_y, to_far), (cross, 1 - side_g, to_cross), (near, 2 + side_y, to_near)):
        for h in range(4):
            rows = p_blocks[asked[0, row, h]]
            out[h, 0:64] = rows[:, 0:128]
            out[h, 64:96] = jnp.concatenate([rows[0:32, 128:192], rows[32:64, 128:192]], axis=1)


def fetch(*refs):
    count = (len(refs) - 1) // 2
    copies = [pltpu.make_async_copy(refs[n], refs[count + n], refs[-1].at[n]) for n in range(count)]
    for copy in copies:
        copy.start()
    for copy in copies:
        copy.wait()


def turned(pair):
    return jnp.concatenate([pair[:, 64:128], pair[:, 0:64]], axis=1)


def spread(pair, last, right, index):
    low = lax.broadcasted_iota(jnp.int32, (64, 128), 1) < 64
    zero = jnp.zeros_like(pair)
    other = turned(pair)
    for p, first, second in ((0, pair, other), (1, other, pair)):
        right[index, p, 0:64] = jnp.where(low, first, zero)
        right[index, p, 64:128] = jnp.where(low, zero, second)
    low, zero, other = low[0:32], zero[0:32], turned(last)
    right[index, 2, 0:32] = jnp.where(low, last, zero)
    right[index, 2, 32:64] = jnp.where(low, other, zero)
    right[index, 2, 64:96] = jnp.where(low, zero, other)
    right[index, 2, 96:128] = jnp.where(low, zero, last)


def spread_rows(rows, right, index):
    last = jnp.concatenate([rows[0:32, 128:192], rows[32:64, 128:192]], axis=1)
    spread(rows[:, 0:128], last, right, index)


def add_pairs(pairs, places, t_slot, left, right, sums):
    for pair in pairs:
        i, a = pair >> 3, pair & 7
        slot = places[a, i]
        wide = jnp.concatenate([right[slot, p] for p in range(3)], axis=1)
        value = jnp.dot(left[pair], wide, preferred_element_type=F32)
        for q in range(3):
            first = places[7 + q, i]
            for p in range(3):
                where = first + t_slot[q, p, a, i]
                sums[p][where] = sums[p][where] + value[q * HALF : (q + 1) * HALF, p * 128 : (p + 1) * 128]


def later_pairs(lists, b):
    sent_far, shift_sent, going, kept_far, shift_kept = (lists[4, n] for n in range(5))
    pairs = []
    for j in range(GROUP):
        k = b * GROUP + j
        m = k - going
        row = jnp.where(k < sent_far, 2, jnp.where(m < 0, 0, jnp.where(m < kept_far, 3, 1)))
        near = jnp.where(k < sent_far, k, k + shift_sent)
        column = jnp.where(m < 0, near, jnp.where(m < kept_far, m, m + shift_kept))
        pairs.append(lists[row, column])
    return pairs


def early(
    sides, wanted, a_slot, p_cols, a_blocks, p_blocks, chip, after, t_slot,
    left, right, sum0, sum1, sum2, lists, places, held, rows4, sems,
):
    sums = (sum0, sum1, sum2)
    row = 1 - sides[0]
    flip_g, flip_y = 4 * (1 - sides[0]), 4 * (1 - sides[1])
    loads = [pltpu.make_async_copy(a_blocks.at[pl.ds(4 * c, 4)], held.at[pl.ds(4 * c, 4)], sems.at[c]) for c in range(4)]
    pulls = [pltpu.make_async_copy(chip.at[wanted[0, row, h]], rows4.at[h], sems.at[4 + h]) for h in range(4)]
    for copy in loads + pulls:
        copy.start()

    def clear(j, carry):
        for total in sums:
            total[j] = jnp.zeros((HALF, 128), F32)
        return carry

    lax.fori_loop(0, BINS, clear, 0)
    counts = [jnp.int32(0)] * 4
    for c in range(4):
        loads[c].wait()
        for i in range(4 * c, 4 * c + 4):
            rows = p_blocks[i]
            spread_rows(rows, right, i)
            full = lax.dot_general(rows, held[i], (((0,), (0,)), ((), ())), preferred_element_type=F32).astype(BF16)
            top = jnp.concatenate([full[q * 64 : q * 64 + 32] for q in range(3)], axis=0)
            bottom = jnp.concatenate([full[q * 64 + 32 : q * 64 + 64] for q in range(3)], axis=0)
            for q in range(3):
                aim = p_cols[q, i]
                side = ((aim >> 1) - 1) << 2
                side = (side ^ jnp.where(side < 8, flip_g, flip_y)) >> 2
                places[7 + q, i] = KC * jnp.where(aim < OWN, aim, OWN + side)
            sent = jnp.maximum(jnp.maximum(places[7, i], places[8, i]), places[9, i]) >= OWN * KC
            for a in range(7):
                pair = i * 8 + a
                left[pair] = jnp.concatenate([top[:, a * 64 : (a + 1) * 64], bottom[:, a * 64 : (a + 1) * 64]], axis=1)
                slot = a_slot[a, i]
                own = slot < 16
                places[a, i] = jnp.where(own, slot, slot ^ jnp.where(slot < 24, flip_g, flip_y))
                for kind, here in enumerate((own & sent, own & ~sent, ~own & sent, ~own & ~sent)):
                    lists[kind, counts[kind]] = pair
                    counts[kind] = counts[kind] + jnp.where(here, 1, 0)
    groups = jnp.minimum((counts[0] + counts[1]) // GROUP, AHEAD)
    done = groups * GROUP
    lists[4, 0] = counts[2]
    lists[4, 1] = jnp.minimum(done, counts[0]) - counts[2]
    lists[4, 2] = counts[2] + counts[0] - jnp.minimum(done, counts[0])
    lists[4, 3] = counts[3]
    lists[4, 4] = jnp.maximum(done - counts[0], 0) - counts[3]
    lists[4, 5] = 112 // GROUP - groups
    first = counts[0]
    for h in range(4):
        pulls[h].wait()
    for h in range(4):
        spread_rows(rows4[h], right, 16 + h)

    def body(b, carry):
        pairs = []
        for j in range(GROUP):
            k = b * GROUP + j
            head = k < first
            pairs.append(lists[jnp.where(head, 0, 1), jnp.where(head, k, k - first)])
        add_pairs(pairs, places, t_slot, left, right, sums)
        return carry

    lax.fori_loop(0, groups, body, 0)


def outward(
    places, t_slot, lists, left, right_in, s0, s1, s2, cross, near, far, o0, o1, o2, o3, right, sum0, sum1, sum2
):
    for h in range(4):
        for rows, base in ((cross, 20), (near, 24), (far, 28)):
            spread(rows[h, 0:64], rows[h, 64:96], right, base + h)
    going = lists[4, 2]

    def body(b, carry):
        pairs = later_pairs(lists, b)
        add_pairs(pairs, places, t_slot, left, right, (sum0, sum1, sum2))
        return carry

    lax.fori_loop(0, (going + GROUP - 1) // GROUP, body, 0)
    for k, out in enumerate((o0, o1, o2, o3)):
        part = pl.ds((OWN + k) * KC, KC)
        out[...] = (sum0[part] + sum1[part] + sum2[part]).astype(BF16)


def inward(places, t_slot, lists, left, right, s0, s1, s2, out, sum0, sum1, sum2):
    going = lists[4, 2]

    def body(b, carry):
        pairs = later_pairs(lists, b)
        add_pairs(pairs, places, t_slot, left, right, (sum0, sum1, sum2))
        return carry

    lax.fori_loop((going + GROUP - 1) // GROUP, lists[4, 5], body, 0)
    part = pl.ds(0, OWN * KC)
    out[...] = sum0[part] + sum1[part] + sum2[part]


def finish(own, r0, r1, r2, r3, out):
    for c in range(OWN):
        for s in range(KC):
            value = own[c * KC + s]
            if c == 0:
                for r in (r0, r1, r2, r3):
                    value = value + r[s].astype(F32)
            out[c, 0:HALF, s * 64 : (s + 1) * 64] = value[:, 0:64]
            out[c, HALF:64, s * 64 : (s + 1) * 64] = value[:, 64:128]


def shards(a_blocks, p_blocks, a_slot, halo_rows, p_cols, t_slot):
    side_g = lax.axis_index("gx") % 2
    side_y = lax.axis_index("yz") % 2
    sides = jnp.stack([side_g, side_y]).astype(jnp.int32)
    far_ask = swapped(halo_rows, "yz", 1)
    cross_ask = swapped(halo_rows, "gx", 1)
    near_ask = swapped(halo_rows, "yz", 0)
    chip = swapped(p_blocks, "gx", 0)

    sources = [p_blocks, halo_rows, a_slot.T, p_cols.T, t_slot.transpose(1, 3, 2, 0)]
    held, wanted, a_slot, p_cols, t_slot = pl.pallas_call(
        fetch, out_shape=[jax.ShapeDtypeStruct(x.shape, x.dtype) for x in sources],
        in_specs=[HBM] * 5, out_specs=[VMEM] * 5, scratch_shapes=[pltpu.SemaphoreType.DMA((5,))],
        compiler_params=params(2), cost_estimate=cost(0, 800000), name="fetch",
    )(*[pltpu.with_memory_space_constraint(x, pltpu.HBM) for x in sources])
    piece = jax.ShapeDtypeStruct((4, 96, 128), BF16)
    to_cross, to_near, to_far = pl.pallas_call(
        gather_rows, out_shape=[piece] * 3, in_specs=[SMEM] * 4 + [VMEM], out_specs=[VMEM] * 3,
        compiler_params=params(2), cost_estimate=cost(0, 700000), name="gather_rows",
    )(sides, cross_ask, near_ask, far_ask, held)
    far = swapped(to_far, "yz", 1)
    cross = swapped(to_cross, "gx", 1)
    near = swapped(to_near, "yz", 0)

    left, right, *sums, lists, places = pl.pallas_call(
        early,
        out_shape=[LEFT, RIGHT] + SUMS + [jax.ShapeDtypeStruct((5, 128), jnp.int32), jax.ShapeDtypeStruct((10, 16), jnp.int32)],
        in_specs=[SMEM] * 4 + [HBM, VMEM, ANY, ANY, SMEM], out_specs=[VMEM] * 5 + [SMEM] * 2,
        scratch_shapes=[
            pltpu.VMEM((16, 64, 448), BF16), pltpu.VMEM((4, 64, 192), BF16),
            pltpu.SemaphoreType.DMA((8,)),
        ],
        compiler_params=params(), cost_estimate=cost(400000000, 6000000), name="early",
    )(
        sides, wanted, a_slot, p_cols, pltpu.with_memory_space_constraint(a_blocks, pltpu.HBM), held, chip, to_far, t_slot,
    )

    packed = jax.ShapeDtypeStruct((KC, HALF, 128), BF16)
    *outs, right, sum0, sum1, sum2 = pl.pallas_call(
        outward,
        out_shape=[packed] * 4 + [RIGHT] + SUMS,
        in_specs=[SMEM] * 3 + [VMEM] * 8, out_specs=[VMEM] * 8,
        input_output_aliases={4: 4, 5: 5, 6: 6, 7: 7},
        compiler_params=params(), cost_estimate=cost(400000000, 6000000), name="outward",
    )(places, t_slot, lists, left, right, *sums, cross, near, far)
    got = [
        swapped(outs[0], "gx", 0), swapped(outs[1], "gx", 1),
        swapped(outs[2], "yz", 0), swapped(outs[3], "yz", 1),
    ]

    own, *_ = pl.pallas_call(
        inward,
        out_shape=[jax.ShapeDtypeStruct((OWN * KC, HALF, 128), F32)] + SUMS,
        in_specs=[SMEM] * 3 + [VMEM] * 5, out_specs=[VMEM] * 4,
        input_output_aliases={5: 1, 6: 2, 7: 3},
        compiler_params=params(), cost_estimate=cost(1000000000, 8000000), name="inward",
    )(places, t_slot, lists, left, right, sum0, sum1, sum2)

    return pl.pallas_call(
        finish,
        out_shape=jax.ShapeDtypeStruct((OWN, 64, KC * 64), F32),
        in_specs=[VMEM] * 5, out_specs=VMEM,
        compiler_params=params(4), cost_estimate=cost(0, 1000000), name="finish",
    )(own, *got)


def solution(mesh):
    placed = (
        P(("gx", "yz"), None, None),
        P(("gx", "yz"), None, None),
        P(("gx", "yz"), None),
        P(("gx", "yz"), None, None),
        P(("gx", "yz"), None),
        P(("gx", "yz"), None, None, None),
    )
    return jax.shard_map(shards, mesh=mesh, in_specs=placed, out_specs=P(("gx", "yz"), None, None), check_vma=False)
```

```python
import jax
import jax.numpy as jnp
from jax import lax
from jax.experimental import pallas as pl
from jax.experimental.pallas import tpu as pltpu
from jax.sharding import PartitionSpec as P


KC = 9
HALF = 32
OWN = 2
BINS = 6 * KC
F32 = jnp.float32
BF16 = jnp.bfloat16
VMEM = pl.BlockSpec(memory_space=pltpu.VMEM)
SMEM = pl.BlockSpec(memory_space=pltpu.SMEM)
ANY = pl.BlockSpec(memory_space=pl.ANY)
HBM = pl.BlockSpec(memory_space=pltpu.HBM)
GROUP = 14
AHEAD = 2
I32 = jnp.int32
LEFT = jax.ShapeDtypeStruct((112, 96, 128), BF16)
RIGHT = jax.ShapeDtypeStruct((32, 3, 128, 128), BF16)
SUMS = [jax.ShapeDtypeStruct((BINS, HALF, 128), F32)] * 3


def params(mib=16):
    return pltpu.CompilerParams(vmem_limit_bytes=mib << 20)


def cost(flops, moved):
    return pl.CostEstimate(flops=flops, bytes_accessed=moved, transcendentals=0)


def swapped(value, axis, odd):
    count = lax.axis_size(axis)
    pairs = []
    for low in range(odd, count + odd, 2):
        first, second = low % count, (low + 1) % count
        pairs += [(first, second), (second, first)]
    return lax.ppermute(value, axis, pairs)


def gather_rows(sides, cross, near, far, p_blocks, to_cross, to_near, to_far):
    side_g, side_y = sides[0], sides[1]
    for asked, row, out in ((far, 3 - side_y, to_far), (cross, 1 - side_g, to_cross), (near, 2 + side_y, to_near)):
        for h in range(4):
            rows = p_blocks[asked[0, row, h]]
            out[h, 0:64] = rows[:, 0:128]
            out[h, 64:96] = jnp.concatenate([rows[0:32, 128:192], rows[32:64, 128:192]], axis=1)


def fetch(*refs):
    count = (len(refs) - 1) // 2
    copies = [pltpu.make_async_copy(refs[n], refs[count + n], refs[-1].at[n]) for n in range(count)]
    for copy in copies:
        copy.start()
    for copy in copies:
        copy.wait()


def turned(pair):
    return jnp.concatenate([pair[:, 64:128], pair[:, 0:64]], axis=1)


def spread(pair, last, right, index):
    low = lax.broadcasted_iota(jnp.int32, (64, 128), 1) < 64
    zero = jnp.zeros_like(pair)
    other = turned(pair)
    for p, first, second in ((0, pair, other), (1, other, pair)):
        right[index, p, 0:64] = jnp.where(low, first, zero)
        right[index, p, 64:128] = jnp.where(low, zero, second)
    low, zero, other = low[0:32], zero[0:32], turned(last)
    right[index, 2, 0:32] = jnp.where(low, last, zero)
    right[index, 2, 32:64] = jnp.where(low, other, zero)
    right[index, 2, 64:96] = jnp.where(low, zero, other)
    right[index, 2, 96:128] = jnp.where(low, zero, last)


def spread_rows(rows, right, index):
    last = jnp.concatenate([rows[0:32, 128:192], rows[32:64, 128:192]], axis=1)
    spread(rows[:, 0:128], last, right, index)


def add_pairs(pairs, bins, slots, left, right, sums):
    for pair in pairs:
        i, a = pair & 15, pair >> 4
        slot = slots[a, i]
        wide = jnp.concatenate([right[slot, p] for p in range(3)], axis=1)
        value = jnp.dot(left[pair], wide, preferred_element_type=F32)
        for q in range(3):
            for p in range(3):
                where = bins[q, p, a, i]
                sums[p][where] = sums[p][where] + value[q * HALF : (q + 1) * HALF, p * 128 : (p + 1) * 128]


def arrange(sides, a_slot, p_cols, t_slot, order, bins, slots):
    flip_g, flip_y = 4 * (1 - sides[0]), 4 * (1 - sides[1])
    slot, aim = a_slot[...], p_cols[...]
    slots[...] = jnp.where(slot < 16, slot, slot ^ jnp.where(slot < 24, flip_g, flip_y))
    side = ((aim >> 1) - 1) << 2
    side = (side ^ jnp.where(side < 8, flip_g, flip_y)) >> 2
    target = KC * jnp.where(aim < OWN, aim, OWN + side)
    for q in range(3):
        for p in range(3):
            bins[q, p] = t_slot[q, p] + target[q : q + 1]

    top = jnp.maximum(jnp.maximum(aim[0:1], aim[1:2]), aim[2:3])
    unused = jnp.full((1, 16), 1000, I32)
    flat = jnp.concatenate([slot[a : a + 1] for a in range(7)] + [unused], axis=1)
    tops = jnp.concatenate([top] * 8, axis=1)
    real, own, sent = flat < 1000, flat < 16, tops >= OWN
    one = lambda mask: jnp.where(mask, 1.0, 0.0).astype(F32)
    kinds = [one(own & sent), one(own & ~sent), one(real & ~own & sent), one(real & ~own & ~sent)]
    kinds = jnp.concatenate(kinds + [jnp.zeros((4, 128), F32)], axis=0).astype(BF16)
    down = lax.broadcasted_iota(I32, (128, 128), 0)
    across = lax.broadcasted_iota(I32, (128, 128), 1)
    before = jnp.where(down < across, 1.0, 0.0).astype(BF16)
    rank = jnp.dot(kinds, before, preferred_element_type=F32)
    total = jnp.dot(kinds, jnp.ones((128, 128), BF16), preferred_element_type=F32)
    n0, n1, n2, n3 = total[0:1], total[1:2], total[2:3], total[3:4]
    done = jnp.minimum(jnp.floor((n0 + n1) * (1.0 / GROUP) + 0.25 / GROUP), AHEAD) * GROUP
    head = jnp.minimum(n0, done)
    tail = done - head
    going = done + n2 + n0 - head
    r0, r1, r2, r3 = rank[0:1], rank[1:2], rank[2:3], rank[3:4]
    place = jnp.where(r0 < head, r0, done + n2 + r0 - head) * kinds[0:1].astype(F32)
    place = place + jnp.where(r1 < tail, head + r1, going + n3 + r1 - tail) * kinds[1:2].astype(F32)
    place = place + (done + r2) * kinds[2:3].astype(F32) + (going + r3) * kinds[3:4].astype(F32)
    place = jnp.where(real, place.astype(I32), across[0:1])
    hit = jnp.where(down == place, 1.0, 0.0).astype(BF16)
    names = across[0:8].astype(F32).astype(BF16)
    found = lax.dot_general(names, hit, (((1,), (1,)), ((), ())), preferred_element_type=F32)
    rows = lax.broadcasted_iota(I32, (8, 128), 0)
    order[...] = jnp.where(rows == 0, found, jnp.where(rows == 1, done, going)).astype(I32)


def early(
    sides, wanted, a_slot, p_cols, a_blocks, p_blocks, chip, after, t_slot,
    left, right, sum0, sum1, sum2, order, bins, slots, held, rows4, order_s, bins_s, slots_s, sems,
):
    sums = (sum0, sum1, sum2)
    row = 1 - sides[0]
    loads = [pltpu.make_async_copy(a_blocks.at[pl.ds(4 * c, 4)], held.at[pl.ds(4 * c, 4)], sems.at[c]) for c in range(4)]
    pulls = [pltpu.make_async_copy(chip.at[wanted[0, row, h]], rows4.at[h], sems.at[4 + h]) for h in range(4)]
    for copy in loads + pulls:
        copy.start()
    arrange(sides, a_slot, p_cols, t_slot, order, bins, slots)
    tables = [
        pltpu.make_async_copy(source, out, sems.at[8 + n])
        for n, (source, out) in enumerate(((order, order_s), (bins, bins_s), (slots, slots_s)))
    ]
    for copy in tables:
        copy.start()

    def clear(j, carry):
        for total in sums:
            total[j] = jnp.zeros((HALF, 128), F32)
        return carry

    lax.fori_loop(0, BINS, clear, 0)
    for c in range(4):
        loads[c].wait()
        for i in range(4 * c, 4 * c + 4):
            rows = p_blocks[i]
            spread_rows(rows, right, i)
            full = lax.dot_general(rows, held[i], (((0,), (0,)), ((), ())), preferred_element_type=F32).astype(BF16)
            top = jnp.concatenate([full[q * 64 : q * 64 + 32] for q in range(3)], axis=0)
            bottom = jnp.concatenate([full[q * 64 + 32 : q * 64 + 64] for q in range(3)], axis=0)
            for a in range(7):
                left[a * 16 + i] = jnp.concatenate([top[:, a * 64 : (a + 1) * 64], bottom[:, a * 64 : (a + 1) * 64]], axis=1)
    for copy in pulls + tables:
        copy.wait()
    for h in range(4):
        spread_rows(rows4[h], right, 16 + h)

    def body(b, carry):
        add_pairs([order_s[0, b * GROUP + j] for j in range(GROUP)], bins_s, slots_s, left, right, sums)
        return carry

    lax.fori_loop(0, order_s[1, 0] // GROUP, body, 0)


def outward(
    bins, slots, order, left, right_in, s0, s1, s2, cross, near, far, o0, o1, o2, o3, right, sum0, sum1, sum2
):
    for h in range(4):
        for rows, base in ((cross, 20), (near, 24), (far, 28)):
            spread(rows[h, 0:64], rows[h, 64:96], right, base + h)

    def body(b, carry):
        add_pairs([order[0, b * GROUP + j] for j in range(GROUP)], bins, slots, left, right, (sum0, sum1, sum2))
        return carry

    lax.fori_loop(order[1, 0] // GROUP, (order[2, 0] + GROUP - 1) // GROUP, body, 0)
    for k, out in enumerate((o0, o1, o2, o3)):
        part = pl.ds((OWN + k) * KC, KC)
        out[...] = (sum0[part] + sum1[part] + sum2[part]).astype(BF16)


def inward(bins, slots, order, left, right, s0, s1, s2, out, sum0, sum1, sum2):
    def body(b, carry):
        add_pairs([order[0, b * GROUP + j] for j in range(GROUP)], bins, slots, left, right, (sum0, sum1, sum2))
        return carry

    lax.fori_loop((order[2, 0] + GROUP - 1) // GROUP, 112 // GROUP, body, 0)
    part = pl.ds(0, OWN * KC)
    out[...] = sum0[part] + sum1[part] + sum2[part]


def finish(own, r0, r1, r2, r3, out):
    for c in range(OWN):
        for s in range(KC):
            value = own[c * KC + s]
            if c == 0:
                for r in (r0, r1, r2, r3):
                    value = value + r[s].astype(F32)
            out[c, 0:HALF, s * 64 : (s + 1) * 64] = value[:, 0:64]
            out[c, HALF:64, s * 64 : (s + 1) * 64] = value[:, 64:128]


def shards(a_blocks, p_blocks, a_slot, halo_rows, p_cols, t_slot):
    side_g = lax.axis_index("gx") % 2
    side_y = lax.axis_index("yz") % 2
    sides = jnp.stack([side_g, side_y]).astype(jnp.int32)
    far_ask = swapped(halo_rows, "yz", 1)
    cross_ask = swapped(halo_rows, "gx", 1)
    near_ask = swapped(halo_rows, "yz", 0)
    chip = swapped(p_blocks, "gx", 0)

    sources = [p_blocks, halo_rows, a_slot.T, p_cols.T, t_slot.transpose(1, 3, 2, 0)]
    held, wanted, a_slot, p_cols, t_slot = pl.pallas_call(
        fetch, out_shape=[jax.ShapeDtypeStruct(x.shape, x.dtype) for x in sources],
        in_specs=[HBM] * 5, out_specs=[VMEM] * 5, scratch_shapes=[pltpu.SemaphoreType.DMA((5,))],
        compiler_params=params(2), cost_estimate=cost(0, 800000), name="fetch",
    )(*[pltpu.with_memory_space_constraint(x, pltpu.HBM) for x in sources])
    piece = jax.ShapeDtypeStruct((4, 96, 128), BF16)
    to_cross, to_near, to_far = pl.pallas_call(
        gather_rows, out_shape=[piece] * 3, in_specs=[SMEM] * 4 + [VMEM], out_specs=[VMEM] * 3,
        compiler_params=params(2), cost_estimate=cost(0, 700000), name="gather_rows",
    )(sides, cross_ask, near_ask, far_ask, held)
    far = swapped(to_far, "yz", 1)
    cross = swapped(to_cross, "gx", 1)
    near = swapped(to_near, "yz", 0)

    left, right, *sums, order, bins, slots = pl.pallas_call(
        early,
        out_shape=[LEFT, RIGHT] + SUMS + [
            jax.ShapeDtypeStruct((8, 128), I32), jax.ShapeDtypeStruct((3, 3, 7, 16), I32), jax.ShapeDtypeStruct((7, 16), I32),
        ],
        in_specs=[SMEM] * 2 + [VMEM] * 2 + [HBM, VMEM, ANY, ANY, VMEM], out_specs=[VMEM] * 8,
        scratch_shapes=[
            pltpu.VMEM((16, 64, 448), BF16), pltpu.VMEM((4, 64, 192), BF16),
            pltpu.SMEM((8, 128), I32), pltpu.SMEM((3, 3, 7, 16), I32), pltpu.SMEM((7, 16), I32), pltpu.SemaphoreType.DMA((11,)),
        ],
        compiler_params=params(), cost_estimate=cost(400000000, 6000000), name="early",
    )(
        sides, wanted, a_slot, p_cols, pltpu.with_memory_space_constraint(a_blocks, pltpu.HBM), held, chip, to_far, t_slot,
    )

    packed = jax.ShapeDtypeStruct((KC, HALF, 128), BF16)
    *outs, right, sum0, sum1, sum2 = pl.pallas_call(
        outward,
        out_shape=[packed] * 4 + [RIGHT] + SUMS,
        in_specs=[SMEM] * 3 + [VMEM] * 8, out_specs=[VMEM] * 8,
        input_output_aliases={4: 4, 5: 5, 6: 6, 7: 7},
        compiler_params=params(), cost_estimate=cost(400000000, 6000000), name="outward",
    )(bins, slots, order, left, right, *sums, cross, near, far)
    got = [
        swapped(outs[0], "gx", 0), swapped(outs[1], "gx", 1),
        swapped(outs[2], "yz", 0), swapped(outs[3], "yz", 1),
    ]

    own, *_ = pl.pallas_call(
        inward,
        out_shape=[jax.ShapeDtypeStruct((OWN * KC, HALF, 128), F32)] + SUMS,
        in_specs=[SMEM] * 3 + [VMEM] * 5, out_specs=[VMEM] * 4,
        input_output_aliases={5: 1, 6: 2, 7: 3},
        compiler_params=params(), cost_estimate=cost(1000000000, 8000000), name="inward",
    )(bins, slots, order, left, right, sum0, sum1, sum2)

    return pl.pallas_call(
        finish,
        out_shape=jax.ShapeDtypeStruct((OWN, 64, KC * 64), F32),
        in_specs=[VMEM] * 5, out_specs=VMEM,
        compiler_params=params(4), cost_estimate=cost(0, 1000000), name="finish",
    )(own, *got)


def solution(mesh):
    placed = (
        P(("gx", "yz"), None, None),
        P(("gx", "yz"), None, None),
        P(("gx", "yz"), None),
        P(("gx", "yz"), None, None),
        P(("gx", "yz"), None),
        P(("gx", "yz"), None, None, None),
    )
    return jax.shard_map(shards, mesh=mesh, in_specs=placed, out_specs=P(("gx", "yz"), None, None), check_vma=False)
```

```python
import jax
import jax.numpy as jnp
from jax import lax
from jax.experimental import pallas as pl
from jax.experimental.pallas import tpu as pltpu
from jax.sharding import PartitionSpec as P


KC = 9
HALF = 32
OWN = 2
BINS = 6 * KC
F32 = jnp.float32
BF16 = jnp.bfloat16
VMEM = pl.BlockSpec(memory_space=pltpu.VMEM)
SMEM = pl.BlockSpec(memory_space=pltpu.SMEM)
ANY = pl.BlockSpec(memory_space=pl.ANY)
HBM = pl.BlockSpec(memory_space=pltpu.HBM)
GROUP = 14
AHEAD = 2
I32 = jnp.int32
LEFT = jax.ShapeDtypeStruct((112, 96, 128), BF16)
RIGHT = jax.ShapeDtypeStruct((32, 3, 128, 128), BF16)
SUMS = [jax.ShapeDtypeStruct((BINS, HALF, 128), F32)] * 3


def params(mib=16):
    return pltpu.CompilerParams(vmem_limit_bytes=mib << 20)


def cost(flops, moved):
    return pl.CostEstimate(flops=flops, bytes_accessed=moved, transcendentals=0)


def swapped(value, axis, odd):
    count = lax.axis_size(axis)
    pairs = []
    for low in range(odd, count + odd, 2):
        first, second = low % count, (low + 1) % count
        pairs += [(first, second), (second, first)]
    return lax.ppermute(value, axis, pairs)


def gather_rows(sides, cross, near, far, p_blocks, to_cross, to_near, to_far):
    side_g, side_y = sides[0], sides[1]
    for asked, row, out in ((far, 3 - side_y, to_far), (cross, 1 - side_g, to_cross), (near, 2 + side_y, to_near)):
        for h in range(4):
            rows = p_blocks[asked[0, row, h]]
            out[h, 0:64] = rows[:, 0:128]
            out[h, 64:96] = jnp.concatenate([rows[0:32, 128:192], rows[32:64, 128:192]], axis=1)


def fetch(*refs):
    count = (len(refs) - 1) // 2
    sems = refs[-1]
    copies = [
        pltpu.make_async_copy(refs[0].at[pl.ds(2 * n, 2)], refs[count].at[pl.ds(2 * n, 2)], sems.at[n]) for n in range(8)
    ]
    copies += [pltpu.make_async_copy(refs[n], refs[count + n], sems.at[7 + n]) for n in range(1, count)]
    for copy in copies:
        copy.start()
    for copy in copies:
        copy.wait()


def turned(pair):
    return jnp.concatenate([pair[:, 64:128], pair[:, 0:64]], axis=1)


def spread(pair, last, right, index):
    low = lax.broadcasted_iota(jnp.int32, (64, 128), 1) < 64
    zero = jnp.zeros_like(pair)
    other = turned(pair)
    for p, first, second in ((0, pair, other), (1, other, pair)):
        right[index, p, 0:64] = jnp.where(low, first, zero)
        right[index, p, 64:128] = jnp.where(low, zero, second)
    low, zero, other = low[0:32], zero[0:32], turned(last)
    right[index, 2, 0:32] = jnp.where(low, last, zero)
    right[index, 2, 32:64] = jnp.where(low, other, zero)
    right[index, 2, 64:96] = jnp.where(low, zero, other)
    right[index, 2, 96:128] = jnp.where(low, zero, last)


def spread_rows(rows, right, index):
    last = jnp.concatenate([rows[0:32, 128:192], rows[32:64, 128:192]], axis=1)
    spread(rows[:, 0:128], last, right, index)


def add_pairs(pairs, bins, slots, left, right, sums):
    for pair in pairs:
        i, a = pair & 15, pair >> 4
        slot = slots[a, i]
        wide = jnp.concatenate([right[slot, p] for p in range(3)], axis=1)
        value = jnp.dot(left[pair], wide, preferred_element_type=F32)
        for q in range(3):
            for p in range(3):
                where = bins[q, p, a, i]
                sums[p][where] = sums[p][where] + value[q * HALF : (q + 1) * HALF, p * 128 : (p + 1) * 128]


def arrange(sides, a_slot, p_cols, t_slot, order, bins, slots):
    flip_g, flip_y = 4 * (1 - sides[0]), 4 * (1 - sides[1])
    slot, aim = a_slot[...], p_cols[...]
    slots[...] = jnp.where(slot < 16, slot, slot ^ jnp.where(slot < 24, flip_g, flip_y))
    side = ((aim >> 1) - 1) << 2
    side = (side ^ jnp.where(side < 8, flip_g, flip_y)) >> 2
    target = KC * jnp.where(aim < OWN, aim, OWN + side)
    for q in range(3):
        for p in range(3):
            bins[q, p] = t_slot[q, p] + target[q : q + 1]

    top = jnp.maximum(jnp.maximum(aim[0:1], aim[1:2]), aim[2:3])
    unused = jnp.full((1, 16), 1000, I32)
    flat = jnp.concatenate([slot[a : a + 1] for a in range(7)] + [unused], axis=1)
    tops = jnp.concatenate([top] * 8, axis=1)
    real, own, sent = flat < 1000, flat < 16, tops >= OWN
    one = lambda mask: jnp.where(mask, 1.0, 0.0).astype(F32)
    kinds = [one(own & sent), one(own & ~sent), one(real & ~own & sent), one(real & ~own & ~sent)]
    kinds = jnp.concatenate(kinds + [jnp.zeros((4, 128), F32)], axis=0).astype(BF16)
    down = lax.broadcasted_iota(I32, (128, 128), 0)
    across = lax.broadcasted_iota(I32, (128, 128), 1)
    before = jnp.where(down < across, 1.0, 0.0).astype(BF16)
    rank = jnp.dot(kinds, before, preferred_element_type=F32)
    total = jnp.dot(kinds, jnp.ones((128, 128), BF16), preferred_element_type=F32)
    n0, n1, n2, n3 = total[0:1], total[1:2], total[2:3], total[3:4]
    done = jnp.minimum(jnp.floor((n0 + n1) * (1.0 / GROUP) + 0.25 / GROUP), AHEAD) * GROUP
    head = jnp.minimum(n0, done)
    tail = done - head
    going = done + n2 + n0 - head
    r0, r1, r2, r3 = rank[0:1], rank[1:2], rank[2:3], rank[3:4]
    place = jnp.where(r0 < head, r0, done + n2 + r0 - head) * kinds[0:1].astype(F32)
    place = place + jnp.where(r1 < tail, head + r1, going + n3 + r1 - tail) * kinds[1:2].astype(F32)
    place = place + (done + r2) * kinds[2:3].astype(F32) + (going + r3) * kinds[3:4].astype(F32)
    place = jnp.where(real, place.astype(I32), across[0:1])
    hit = jnp.where(down == place, 1.0, 0.0).astype(BF16)
    names = across[0:8].astype(F32).astype(BF16)
    found = lax.dot_general(names, hit, (((1,), (1,)), ((), ())), preferred_element_type=F32)
    rows = lax.broadcasted_iota(I32, (8, 128), 0)
    order[...] = jnp.where(rows == 0, found, jnp.where(rows == 1, done, going)).astype(I32)


def early(
    sides, wanted, a_slot, p_cols, a_blocks, p_blocks, chip, after, t_slot,
    left, right, sum0, sum1, sum2, order, bins, slots, held, rows4, order_s, bins_s, slots_s, sems,
):
    sums = (sum0, sum1, sum2)
    row = 1 - sides[0]
    loads = [pltpu.make_async_copy(a_blocks.at[pl.ds(4 * c, 4)], held.at[pl.ds(4 * c, 4)], sems.at[c]) for c in range(4)]
    pulls = [pltpu.make_async_copy(chip.at[wanted[0, row, h]], rows4.at[h], sems.at[4 + h]) for h in range(4)]
    for copy in loads + pulls:
        copy.start()
    arrange(sides, a_slot, p_cols, t_slot, order, bins, slots)
    tables = [
        pltpu.make_async_copy(source, out, sems.at[8 + n])
        for n, (source, out) in enumerate(((order, order_s), (bins, bins_s), (slots, slots_s)))
    ]
    for copy in tables:
        copy.start()

    def clear(j, carry):
        for total in sums:
            total[j] = jnp.zeros((HALF, 128), F32)
        return carry

    lax.fori_loop(0, BINS, clear, 0)
    for c in range(4):
        loads[c].wait()
        for i in range(4 * c, 4 * c + 4):
            rows = p_blocks[i]
            spread_rows(rows, right, i)
            full = lax.dot_general(rows, held[i], (((0,), (0,)), ((), ())), preferred_element_type=F32).astype(BF16)
            top = jnp.concatenate([full[q * 64 : q * 64 + 32] for q in range(3)], axis=0)
            bottom = jnp.concatenate([full[q * 64 + 32 : q * 64 + 64] for q in range(3)], axis=0)
            for a in range(7):
                left[a * 16 + i] = jnp.concatenate([top[:, a * 64 : (a + 1) * 64], bottom[:, a * 64 : (a + 1) * 64]], axis=1)
    for copy in pulls + tables:
        copy.wait()
    for h in range(4):
        spread_rows(rows4[h], right, 16 + h)

    def body(b, carry):
        add_pairs([order_s[0, b * GROUP + j] for j in range(GROUP)], bins_s, slots_s, left, right, sums)
        return carry

    lax.fori_loop(0, order_s[1, 0] // GROUP, body, 0)


def outward(
    bins, slots, order, left, right_in, s0, s1, s2, cross, near, far, o0, o1, o2, o3, right, sum0, sum1, sum2
):
    for h in range(4):
        for rows, base in ((cross, 20), (near, 24), (far, 28)):
            spread(rows[h, 0:64], rows[h, 64:96], right, base + h)

    def body(b, carry):
        add_pairs([order[0, b * GROUP + j] for j in range(GROUP)], bins, slots, left, right, (sum0, sum1, sum2))
        return carry

    lax.fori_loop(order[1, 0] // GROUP, (order[2, 0] + GROUP - 1) // GROUP, body, 0)
    for k, out in enumerate((o0, o1, o2, o3)):
        part = pl.ds((OWN + k) * KC, KC)
        out[...] = (sum0[part] + sum1[part] + sum2[part]).astype(BF16)


def inward(bins, slots, order, left, right, s0, s1, s2, out, sum0, sum1, sum2):
    def body(b, carry):
        add_pairs([order[0, b * GROUP + j] for j in range(GROUP)], bins, slots, left, right, (sum0, sum1, sum2))
        return carry

    lax.fori_loop((order[2, 0] + GROUP - 1) // GROUP, 112 // GROUP, body, 0)
    part = pl.ds(0, OWN * KC)
    out[...] = sum0[part] + sum1[part] + sum2[part]


def finish(own, r0, r1, r2, r3, out, built, sems):
    copies = []
    for c in (1, 0):
        for s in range(KC):
            value = own[c * KC + s]
            if c == 0:
                for r in (r0, r1, r2, r3):
                    value = value + r[s].astype(F32)
            built[c, 0:HALF, s * 64 : (s + 1) * 64] = value[:, 0:64]
            built[c, HALF:64, s * 64 : (s + 1) * 64] = value[:, 64:128]
        copies.append(pltpu.make_async_copy(built.at[c], out.at[c], sems.at[c]))
        copies[-1].start()
    for copy in copies:
        copy.wait()


def shards(a_blocks, p_blocks, a_slot, halo_rows, p_cols, t_slot):
    side_g = lax.axis_index("gx") % 2
    side_y = lax.axis_index("yz") % 2
    sides = jnp.stack([side_g, side_y]).astype(jnp.int32)
    far_ask = swapped(halo_rows, "yz", 1)
    cross_ask = swapped(halo_rows, "gx", 1)
    near_ask = swapped(halo_rows, "yz", 0)
    chip = swapped(p_blocks, "gx", 0)

    sources = [p_blocks, halo_rows, a_slot.T, p_cols.T, t_slot.transpose(1, 3, 2, 0)]
    held, wanted, a_slot, p_cols, t_slot = pl.pallas_call(
        fetch, out_shape=[jax.ShapeDtypeStruct(x.shape, x.dtype) for x in sources],
        in_specs=[HBM] * 5, out_specs=[VMEM] * 5, scratch_shapes=[pltpu.SemaphoreType.DMA((12,))],
        compiler_params=params(2), cost_estimate=cost(0, 800000), name="fetch",
    )(*[pltpu.with_memory_space_constraint(x, pltpu.HBM) for x in sources])
    piece = jax.ShapeDtypeStruct((4, 96, 128), BF16)
    to_cross, to_near, to_far = pl.pallas_call(
        gather_rows, out_shape=[piece] * 3, in_specs=[SMEM] * 4 + [VMEM], out_specs=[VMEM] * 3,
        compiler_params=params(2), cost_estimate=cost(0, 700000), name="gather_rows",
    )(sides, cross_ask, near_ask, far_ask, held)
    far = swapped(to_far, "yz", 1)
    cross = swapped(to_cross, "gx", 1)
    near = swapped(to_near, "yz", 0)

    left, right, *sums, order, bins, slots = pl.pallas_call(
        early,
        out_shape=[LEFT, RIGHT] + SUMS + [
            jax.ShapeDtypeStruct((8, 128), I32), jax.ShapeDtypeStruct((3, 3, 7, 16), I32), jax.ShapeDtypeStruct((7, 16), I32),
        ],
        in_specs=[SMEM] * 2 + [VMEM] * 2 + [HBM, VMEM, ANY, ANY, VMEM], out_specs=[VMEM] * 8,
        scratch_shapes=[
            pltpu.VMEM((16, 64, 448), BF16), pltpu.VMEM((4, 64, 192), BF16),
            pltpu.SMEM((8, 128), I32), pltpu.SMEM((3, 3, 7, 16), I32), pltpu.SMEM((7, 16), I32), pltpu.SemaphoreType.DMA((11,)),
        ],
        compiler_params=params(), cost_estimate=cost(400000000, 6000000), name="early",
    )(
        sides, wanted, a_slot, p_cols, pltpu.with_memory_space_constraint(a_blocks, pltpu.HBM), held, chip, to_far, t_slot,
    )

    packed = jax.ShapeDtypeStruct((KC, HALF, 128), BF16)
    *outs, right, sum0, sum1, sum2 = pl.pallas_call(
        outward,
        out_shape=[packed] * 4 + [RIGHT] + SUMS,
        in_specs=[SMEM] * 3 + [VMEM] * 8, out_specs=[VMEM] * 8,
        input_output_aliases={4: 4, 5: 5, 6: 6, 7: 7},
        compiler_params=params(), cost_estimate=cost(400000000, 6000000), name="outward",
    )(bins, slots, order, left, right, *sums, cross, near, far)
    got = [
        swapped(outs[0], "gx", 0), swapped(outs[1], "gx", 1),
        swapped(outs[2], "yz", 0), swapped(outs[3], "yz", 1),
    ]

    own, *_ = pl.pallas_call(
        inward,
        out_shape=[jax.ShapeDtypeStruct((OWN * KC, HALF, 128), F32)] + SUMS,
        in_specs=[SMEM] * 3 + [VMEM] * 5, out_specs=[VMEM] * 4,
        input_output_aliases={5: 1, 6: 2, 7: 3},
        compiler_params=params(), cost_estimate=cost(1000000000, 8000000), name="inward",
    )(bins, slots, order, left, right, sum0, sum1, sum2)

    return pl.pallas_call(
        finish,
        out_shape=jax.ShapeDtypeStruct((OWN, 64, KC * 64), F32),
        in_specs=[VMEM] * 5, out_specs=HBM,
        scratch_shapes=[pltpu.VMEM((OWN, 64, KC * 64), F32), pltpu.SemaphoreType.DMA((OWN,))],
        compiler_params=params(4), cost_estimate=cost(0, 1000000), name="finish",
    )(own, *got)


def solution(mesh):
    placed = (
        P(("gx", "yz"), None, None),
        P(("gx", "yz"), None, None),
        P(("gx", "yz"), None),
        P(("gx", "yz"), None, None),
        P(("gx", "yz"), None),
        P(("gx", "yz"), None, None, None),
    )
    return jax.shard_map(shards, mesh=mesh, in_specs=placed, out_specs=P(("gx", "yz"), None, None), check_vma=False)
```
